32 devices in a mesh: groups: 2 (over y), rows: 16 (over z, x, core).
Axes of the slice: x: 2, y: 2, z: 4, core: 2. Of those that a mesh axis runs over, the one named last changes fastest.
Arguments:
- basis: bfloat16 [16384, 512], P(('groups', 'rows')), parts along dimension 0, may hold values from -1.5 to 1.5
- elem_owned: int32 [256], P('groups'), parts along dimension 0, may hold values from 0 to 127, as said below
- node_order: int32 [256, 64], P('groups'), parts along dimension 0, may hold values from 0 to 63, as said below
- geometry: float32 [256, 3], P('groups'), parts along dimension 0, may hold values from 0.5 to 4
- deriv: bfloat16 [3, 64, 64], replicated, may hold values from -0.75 to 0.75
Outputs:
- relaid: bfloat16 [16384, 512], P(('groups', 'rows')), parts along dimension 0
- reduced: float32 [1024, 1536], P(('groups', 'rows')), parts along dimension 0
The draws below stay inside these ranges and needn't reach their ends.
There are 2 independent parts, one for each index of `groups`. The reference program is written for one: setup_inputs(seed, part) draws one part's arguments, and reference() takes and returns one part's arrays. A program takes and returns all parts, laid end to end along the dimension named above; an argument that names none is the same for every part. Nothing has to cross between parts.
Inputs may be any that keep to these rules, and one draw needn't show every extreme that they name: `elem_owned`: each element appears once; entry i of each device's block of 8 entries is an element whose number modulo 1 equals i modulo 1. `node_order`: each row is a permutation of 0 to 63.
All inputs are finite; a program needn't handle non-finite values.
Results may differ from the reference program's by a relative error of at most 0.0029.
Values may be sent and summed in bfloat16 or wider, within the bound.
No kernel may reach another device: no remote copies, remote signals or barrier semaphores. Data moves between devices by JAX's collectives and lax.ppermute only.
A program may use at most 64 MiB of HBM per device.

```python
import math
import jax
import jax.numpy as jnp
from jax import lax

NP = 64
COLS = 512
EL = 8
E = 128
ROWS_ALL = 8192
RD = 512
MCLS = 1
N_ROWS = 16


def draw_elem_owned(key, part):
    per_class = E // MCLS
    keys = jax.random.split(key, MCLS)
    shuffled = jax.vmap(lambda one_key: jax.random.permutation(one_key, per_class))(keys)
    members = jnp.arange(MCLS)[:, None] + MCLS * shuffled
    members = members.reshape(MCLS, E // EL, EL // MCLS).transpose(1, 2, 0)
    return members.reshape(-1).astype(jnp.int32)


def draw_node_order(key, part):
    keys = jax.random.split(key, E)
    return jax.vmap(lambda one_key: jax.random.permutation(one_key, NP))(keys).astype(jnp.int32)


def block_levels(rng, extent, pieces, low, top_value):
    def one(dim, parts):
        draws = jax.random.uniform(jax.random.fold_in(jax.random.fold_in(rng, 6), dim), (parts,), jnp.float32, low / len(pieces), top_value / len(pieces))
        return jnp.repeat(jnp.exp(draws), extent[dim] // parts).reshape((-1,) + (1,) * (len(extent) - dim - 1))

    gain = one(*pieces[0])
    for cut in pieces[1:]:
        gain = gain * one(*cut)
    return gain


def centred(own_key, dims, scale, limit, cuts=(), dtype=jnp.bfloat16):
    values = jax.random.normal(own_key, dims, jnp.float32) * scale
    if len(cuts) > 0:
        values = block_levels(own_key, dims, cuts, -0.22, 0.18) * values
    return jnp.clip(values, min=-limit, max=limit).astype(dtype)


def setup_inputs(seed: int = 0, part: int = 0) -> dict:
    arg_keys = jax.random.split(jax.random.key(seed), 6)
    part_keys = jax.random.split(jax.random.fold_in(arg_keys[5], part), 6)
    basis = centred(part_keys[0], (ROWS_ALL, COLS), (ROWS_ALL ** -0.25), 1.5, ((0, 16),))
    elem_owned = draw_elem_owned(jax.random.fold_in(jax.random.fold_in(arg_keys[5], part), 71), part)
    node_order = draw_node_order(jax.random.fold_in(jax.random.fold_in(arg_keys[5], part), 71), part)
    geometry = jnp.clip(jnp.exp(jax.random.uniform(part_keys[3], (E, 3), jnp.float32, math.log(0.5), math.log(4.0))), 0.5, 4.0)
    deriv = centred(arg_keys[4], (3, NP, NP), NP ** -0.5, 0.75)
    return {"basis": basis, "elem_owned": elem_owned, "node_order": node_order, "geometry": geometry, "deriv": deriv}


def reference(basis, elem_owned, node_order, geometry, deriv):
    global_node = NP * elem_owned[:, None] + node_order[elem_owned]
    stored = ((global_node % N_ROWS) * RD + global_node // N_ROWS).astype(jnp.int32)
    relaid = basis[stored.reshape(-1)]
    geo_rows = geometry[elem_owned]
    deriv_wide = deriv.astype(jnp.float32)
    blocks_basis = relaid.reshape(N_ROWS, EL, NP, COLS)
    blocks_geo = geo_rows.reshape(N_ROWS, EL, 3)

    def step(total, block):
        block_basis, block_geo = block
        image = jnp.einsum("dkl,elc->ekdc", deriv_wide, block_basis.astype(jnp.float32))
        image = (image * block_geo[:, None, :, None]).astype(jnp.bfloat16)
        image = image.reshape(EL * NP, 3 * COLS)
        flat = block_basis.reshape(EL * NP, COLS)
        term = lax.dot_general(flat, image, (((0,), (0,)), ((), ())), preferred_element_type=jnp.float32)
        return total + term, None

    start = jnp.zeros((COLS, 3 * COLS), jnp.float32)
    reduced, unused = lax.scan(step, start, (blocks_basis, blocks_geo))
    return relaid, reduced
```

```python
import functools

import jax
import jax.numpy as jnp
from jax import lax
from jax.experimental import pallas as pl
from jax.experimental.pallas import tpu as pltpu
from jax.sharding import PartitionSpec as P

NP = 64
QUAD = 4
GRANULE = 16
LANES = (((1,), (1,)), ((), ()))


def whole_vmem(count):
    return [pl.BlockSpec(memory_space=pltpu.VMEM)] * count


def f32_dot(left, right, dims=(((1,), (0,)), ((), ()))):
    return lax.dot_general(left, right, dims, preferred_element_type=jnp.float32)


def call(kernel, outs, args, flops, scratch=(), scalars=0):
    moved = sum(a.size * a.dtype.itemsize for a in args)
    moved += sum(o.size * o.dtype.itemsize for o in outs)
    specs = [pl.BlockSpec(memory_space=pltpu.SMEM)] * scalars
    return pl.pallas_call(
        kernel,
        out_shape=outs,
        in_specs=specs + whole_vmem(len(args) - scalars),
        out_specs=whole_vmem(len(outs)),
        scratch_shapes=scratch,
        cost_estimate=pl.CostEstimate(flops=flops, bytes_accessed=moved, transcendentals=0),
    )(*args)


def pack_kernel(quads, repeats, where_ref, owned_ref, basis_ref, *out_refs):
    total = owned_ref.shape[1]
    rows = basis_ref.shape[0]
    block = rows // quads
    quad_elems = block // repeats
    first = where_ref[0] * quad_elems
    row = lax.broadcasted_iota(jnp.int32, (rows, total), 0)
    slot = lax.broadcasted_iota(jnp.int32, (rows, total), 1)
    wanted = row // repeats + first
    wanted = jnp.where(wanted >= total, wanted - total, wanted)
    pick = (wanted == slot).astype(jnp.float32).astype(jnp.bfloat16)
    owned = owned_ref[...]
    parts = jnp.concatenate(
        [(owned % NP).astype(jnp.float32), (owned // NP).astype(jnp.float32), jnp.zeros((6, total), jnp.float32)], axis=0
    ).astype(jnp.bfloat16)
    found = f32_dot(pick, parts, LANES)
    elem = (found[:, 0:1] + NP * found[:, 1:2]).astype(jnp.int32)
    index = elem * repeats + lax.broadcasted_iota(jnp.int32, (rows, 1), 0) % repeats
    column = lax.broadcasted_iota(jnp.int32, (rows, rows), 1)
    onehot = (index == column).astype(jnp.float32).astype(jnp.bfloat16)
    moved = f32_dot(onehot, basis_ref[...]).astype(jnp.bfloat16)
    for k in range(quads):
        out_refs[k][...] = moved[k * block : (k + 1) * block]


def prepare_kernel(slot_ref, wide_ref, out_ref):
    groups, size = slot_ref.shape
    row = lax.broadcasted_iota(jnp.int32, (size, size), 0)
    for g in range(groups):
        onehot = (row == slot_ref[g : g + 1, :]).astype(jnp.float32).astype(jnp.bfloat16)
        for d in range(3):
            half = f32_dot(onehot, wide_ref[d]).astype(jnp.bfloat16)
            out_ref[g, d] = f32_dot(half, onehot, LANES).astype(jnp.bfloat16)


def group_rows(pieces, start):
    return jnp.concatenate([piece[pl.ds(start, GRANULE), :] for piece in pieces], axis=0)


def product_kernel(pieces_count, quads, *refs):
    pieces = refs[:pieces_count]
    select_ref, matrix_ref, scale_ref = refs[pieces_count : pieces_count + 3]
    own_ref, *send_refs = refs[pieces_count + 3 : pieces_count + 3 + quads]
    left_ref, right_ref = refs[pieces_count + 3 + quads :]
    groups, _, size, _ = matrix_ref.shape
    slab = select_ref.shape[0]
    for g in range(groups):
        rows = group_rows(pieces, g * GRANULE)
        right_ref[g * size : (g + 1) * size, :] = rows
        chosen = f32_dot(select_ref[...], rows, LANES).astype(jnp.bfloat16)
        for d in range(3):
            left = f32_dot(chosen, matrix_ref[g, d]) * scale_ref[g, d : d + 1, :]
            left_ref[d * slab : (d + 1) * slab, g * size : (g + 1) * size] = left.astype(jnp.bfloat16)
    part = slab // quads
    for d in range(3):
        total = f32_dot(left_ref[d * slab : (d + 1) * slab, :], right_ref[...])
        own_ref[d] = total[0:part]
        for k in range(1, quads):
            send_refs[k - 1][d] = total[k * part : (k + 1) * part].astype(jnp.bfloat16)


def relaid_kernel(pieces_count, where_ref, *refs):
    pieces = refs[:pieces_count]
    order_ref, out_ref = refs[pieces_count:]
    own_groups, size, _ = order_ref.shape
    for h in range(own_groups):
        start = pl.multiple_of((where_ref[1] * own_groups + h) * GRANULE, GRANULE)
        rows = group_rows(pieces, start)
        out_ref[h * size : (h + 1) * size, :] = f32_dot(order_ref[h], rows).astype(jnp.bfloat16)


def sum_kernel(own_ref, *refs):
    out_ref = refs[-1]
    columns = own_ref.shape[2]
    for d in range(3):
        total = own_ref[d]
        for ref in refs[:-1]:
            total = total + ref[d].astype(jnp.float32)
        out_ref[:, d * columns : (d + 1) * columns] = total


def by_quads(basis, elem_owned, node_order, geometry, deriv):
    width = lax.axis_size("rows")
    position = lax.axis_index("rows").astype(jnp.int32)
    local_rows, columns = basis.shape
    local_elems = local_rows // NP
    repeats = NP // width
    quads = width // QUAD
    quad, seat = position // QUAD, position % QUAD
    quad_elems = QUAD * local_elems
    block = quad_elems * repeats
    groups = block // GRANULE
    elems = GRANULE // repeats
    size = width * GRANULE
    part = columns // width
    slab = quads * part
    where = jnp.stack([quad, seat])

    piece = jax.ShapeDtypeStruct((block, columns), jnp.bfloat16)
    packed = call(
        functools.partial(pack_kernel, quads, repeats),
        [piece] * quads,
        (where, elem_owned[None, :], basis),
        2 * local_rows * local_rows * columns,
        scalars=1,
    )

    def shift(k):
        return [(i, (i + QUAD * k) % width) for i in range(width)]

    def flip(bit):
        return [(i, i ^ bit) for i in range(width)]

    arrived = [packed[0]] + [lax.ppermute(packed[k], "rows", shift(k)) for k in range(1, quads)]
    pieces = []
    for k in range(quads):
        across = lax.ppermute(arrived[k], "rows", flip(2))
        beside = lax.ppermute(arrived[k], "rows", flip(1))
        corner = lax.ppermute(across, "rows", flip(1))
        pieces += [arrived[k], beside, across, corner]

    quad_owned = lax.dynamic_slice_in_dim(elem_owned, quad * quad_elems, quad_elems)
    orders = node_order[quad_owned]
    source = orders % width
    place = (quad - source // QUAD) % quads * QUAD + ((source % QUAD) ^ seat)
    place = place.reshape(quad_elems, NP)
    inside = (jnp.arange(quad_elems, dtype=jnp.int32) % elems)[:, None] * repeats
    slot = (place * GRANULE + inside + orders // width).reshape(groups, size)
    geo = geometry[quad_owned].reshape(groups, elems, 3).transpose(0, 2, 1)
    scale = jnp.broadcast_to(geo[:, :, None, :, None], (groups, 3, width, elems, repeats)).reshape(groups, 3, size)
    same = jnp.arange(size) // NP
    wide = jnp.where(same[:, None] == same[None, :], jnp.tile(deriv, (1, elems, elems)), jnp.bfloat16(0))
    (matrix,) = call(
        prepare_kernel,
        [jax.ShapeDtypeStruct((groups, 3, size, size), jnp.bfloat16)],
        (slot, wide),
        groups * 3 * 4 * size**3,
    )
    row = jnp.arange(slab, dtype=jnp.int32)
    target = ((quad + row // part) % quads * QUAD + seat) * part + row % part
    select = (target[:, None] == jnp.arange(columns)[None, :]).astype(jnp.bfloat16)

    block_shape = (3, part, columns)
    sums = call(
        functools.partial(product_kernel, width, quads),
        [jax.ShapeDtypeStruct(block_shape, jnp.float32)]
        + [jax.ShapeDtypeStruct(block_shape, jnp.bfloat16)] * (quads - 1),
        (*pieces, select, matrix, scale),
        2 * width * block * slab * 3 * (columns + size) + 2 * width * block * slab * columns,
        scratch=[
            pltpu.VMEM((3 * slab, width * block), jnp.bfloat16),
            pltpu.VMEM((width * block, columns), jnp.bfloat16),
        ],
    )
    landed = [lax.ppermute(sums[k], "rows", shift(k)) for k in range(1, quads)]

    own_groups = groups // QUAD
    own_slot = lax.dynamic_slice_in_dim(slot, seat * own_groups, own_groups)
    order = (own_slot[:, :, None] == jnp.arange(size)[None, None, :]).astype(jnp.bfloat16)
    (relaid,) = call(
        functools.partial(relaid_kernel, width),
        [jax.ShapeDtypeStruct((local_rows, columns), jnp.bfloat16)],
        (where, *pieces, order),
        2 * local_rows * size * columns,
        scalars=1,
    )
    (reduced,) = call(
        sum_kernel,
        [jax.ShapeDtypeStruct((part, 3 * columns), jnp.float32)],
        (sums[0], *landed),
        3 * quads * part * columns,
    )
    return relaid, reduced


def by_rows(basis, elem_owned, node_order, geometry, deriv):
    width_rows = lax.axis_size("rows")
    position = lax.axis_index("rows")
    local_rows, columns = basis.shape
    local_elems = local_rows // NP
    classes = max(1, width_rows // NP)
    repeats = max(1, NP // width_rows)
    class_table = elem_owned.reshape(width_rows, local_elems // classes, classes)
    my_class = position // NP % classes
    chosen = lax.dynamic_index_in_dim(class_table, my_class, axis=2, keepdims=False)
    offsets = position % NP + width_rows * jnp.arange(repeats, dtype=jnp.int32)
    global_node = NP * chosen[:, :, None] + offsets[None, None, :]
    local_index = ((global_node - position) // width_rows).reshape(-1)
    outgoing = basis[local_index]
    arrived = lax.all_to_all(outgoing, "rows", split_axis=0, concat_axis=0, tiled=True)
    my_elems = lax.dynamic_slice_in_dim(elem_owned, position * local_elems, local_elems)
    my_orders = node_order[my_elems]
    my_nodes = NP * my_elems[:, None] + my_orders
    source = my_nodes % width_rows
    within = (jnp.arange(local_elems, dtype=jnp.int32) // classes)[:, None]
    slot_index = (source * (local_elems // classes) + within) * repeats + my_orders // width_rows
    relaid = arrived[slot_index.reshape(-1)]
    geo_rows = geometry[my_elems]
    image = jnp.einsum(
        "dkl,elc->ekdc",
        deriv,
        relaid.reshape(local_elems, NP, columns),
        preferred_element_type=jnp.float32,
    )
    image = (image * geo_rows[:, None, :, None]).astype(jnp.bfloat16)
    image = image.reshape(local_rows, 3 * columns)
    reduced = lax.psum_scatter(
        lax.dot_general(
            relaid, image, (((0,), (0,)), ((), ())), preferred_element_type=jnp.float32
        ),
        "rows",
        scatter_dimension=0,
        tiled=True,
    )
    return (relaid, reduced)


def solution(mesh):
    width = mesh.shape["rows"]
    local = by_quads if width % QUAD == 0 and NP % width == 0 else by_rows
    return jax.shard_map(
        local,
        mesh=mesh,
        in_specs=(
            P(("groups", "rows"), None),
            P("groups"),
            P("groups", None),
            P("groups", None),
            P(),
        ),
        out_specs=(P(("groups", "rows"), None), P(("groups", "rows"), None)),
        check_vma=False,
    )
```

```python
import functools
import math

import jax
import jax.numpy as jnp
from jax import lax
from jax.experimental import pallas as pl
from jax.experimental.pallas import tpu as pltpu
from jax.sharding import PartitionSpec as P

NP = 64
QUAD = 4
GRANULE = 16
KERNEL_BYTES = 16 * 2**20
LANES = (((1,), (1,)), ((), ()))


def whole_vmem(count):
    return [pl.BlockSpec(memory_space=pltpu.VMEM)] * count


def f32_dot(left, right, dims=(((1,), (0,)), ((), ()))):
    return lax.dot_general(left, right, dims, preferred_element_type=jnp.float32)


def near(shape, dtype):
    return pltpu.VMEM(shape, dtype)


def size_of(array):
    return math.prod(array.shape) * jnp.dtype(array.dtype).itemsize


def call(kernel, outs, args, flops, scratch=()):
    moved = sum(size_of(a) for a in (*args, *outs))
    return pl.pallas_call(
        kernel,
        out_shape=outs,
        in_specs=whole_vmem(len(args)),
        out_specs=whole_vmem(len(outs)),
        scratch_shapes=scratch,
        compiler_params=pltpu.CompilerParams(vmem_limit_bytes=KERNEL_BYTES),
        cost_estimate=pl.CostEstimate(flops=flops, bytes_accessed=moved, transcendentals=0),
    )(*(pltpu.with_memory_space_constraint(a, pltpu.VMEM) for a in args))


def one(mask):
    return mask.astype(jnp.float32).astype(jnp.bfloat16)


def iota(shape, axis):
    return lax.broadcasted_iota(jnp.int32, shape, axis)


def seat_and_quad():
    position = lax.axis_index("rows").astype(jnp.int32)
    return position % QUAD, position // QUAD


def pack_kernel(quads, repeats, owned_ref, basis_ref, *out_refs):
    total = owned_ref.shape[1]
    rows = basis_ref.shape[0]
    block = rows // quads
    quad_elems = block // repeats
    quad = seat_and_quad()[1]
    row = iota((rows, total), 0)
    wanted = ((row // block) ^ quad) * quad_elems + row % block // repeats
    pick = one(wanted == iota((rows, total), 1))
    owned = owned_ref[...].astype(jnp.float32)
    high = jnp.floor(owned / NP)
    parts = jnp.concatenate([owned - NP * high, high, jnp.zeros((6, total), jnp.float32)], axis=0)
    found = f32_dot(pick, parts.astype(jnp.bfloat16), LANES)
    elem = (found[:, 0:1] + NP * found[:, 1:2]).astype(jnp.int32)
    index = elem * repeats + iota((rows, 1), 0) % repeats
    onehot = one(index == iota((rows, rows), 1))
    moved = f32_dot(onehot, basis_ref[...]).astype(jnp.bfloat16)
    for k in range(quads):
        out_refs[k][...] = moved[k * block : (k + 1) * block]


def prepare_kernel(width, repeats, owned_ref, order_ref, geo_ref, deriv_ref, matrix_ref, scale_ref, place_ref):
    groups, _, size, _ = matrix_ref.shape
    total = owned_ref.shape[1]
    elems = size // NP
    quad_elems = groups * elems
    seat, quad = seat_and_quad()
    first = quad * quad_elems
    owner = one(iota((total, total), 0) == owned_ref[...])
    row = iota((quad_elems, total), 0)
    mine = one(first + row % groups * elems + row // groups == iota((quad_elems, total), 1))
    chosen = f32_dot(mine, owner, LANES).astype(jnp.bfloat16)
    table = order_ref[...].astype(jnp.float32).astype(jnp.bfloat16)
    orders = f32_dot(chosen, table, LANES).astype(jnp.int32)
    orders = jnp.concatenate([orders[e * groups : (e + 1) * groups] for e in range(elems)], axis=1)
    source = orders % width
    inside = iota((groups, size), 1) // NP * repeats + orders // width
    slot = (((source // QUAD) ^ quad) * QUAD + ((source % QUAD) ^ seat)) * GRANULE + inside

    lane = iota((total, size), 1)
    geo = geo_ref[...]
    top = geo.astype(jnp.bfloat16).astype(jnp.float32)
    middle = (geo - top).astype(jnp.bfloat16).astype(jnp.float32)
    parts = jnp.concatenate([top, middle, geo - top - middle], axis=0).astype(jnp.bfloat16)
    by_slot = f32_dot(parts, owner, (((1,), (0,)), ((), ()))).astype(jnp.bfloat16)
    for g in range(groups):
        stored = first + g * elems + lane % GRANULE // repeats
        spread = f32_dot(by_slot, one(iota((total, size), 0) == stored))
        scale_ref[g] = spread[0:3] + spread[3:6] + spread[6:9]

    same = iota((size, size), 0) // NP == iota((size, size), 1) // NP
    blocks = []
    for d in range(3):
        wide = jnp.concatenate([deriv_ref[d].astype(jnp.float32)] * elems, axis=1)
        tall = jnp.concatenate([wide] * elems, axis=0)
        blocks.append(jnp.where(same, tall, 0.0).astype(jnp.bfloat16))
    for g in range(groups):
        onehot = one(iota((size, size), 0) == slot[g : g + 1, :])
        place_ref[g] = onehot
        for d in range(3):
            half = f32_dot(onehot, blocks[d]).astype(jnp.bfloat16)
            matrix_ref[g, d] = f32_dot(half, onehot, LANES).astype(jnp.bfloat16)


def group_rows(pieces, start):
    return jnp.concatenate([piece[pl.ds(start, GRANULE), :] for piece in pieces], axis=0)


def product_kernel(pieces_count, quads, *refs):
    pieces = refs[:pieces_count]
    matrix_ref, scale_ref = refs[pieces_count : pieces_count + 2]
    own_ref, *send_refs = refs[pieces_count + 2 : pieces_count + 2 + quads]
    left_ref, right_ref = refs[pieces_count + 2 + quads :]
    groups, _, size, _ = matrix_ref.shape
    _, part, columns = own_ref.shape
    slab = quads * part
    seat, quad = seat_and_quad()
    row = iota((slab, columns), 0)
    target = (((row // part) ^ quad) * QUAD + seat) * part + row % part
    select = one(target == iota((slab, columns), 1))
    for g in range(groups):
        rows = group_rows(pieces, g * GRANULE)
        right_ref[g * size : (g + 1) * size, :] = rows
        chosen = f32_dot(select, rows, LANES).astype(jnp.bfloat16)
        for d in range(3):
            left = f32_dot(chosen, matrix_ref[g, d]) * scale_ref[g, d : d + 1, :]
            left_ref[d * slab : (d + 1) * slab, g * size : (g + 1) * size] = left.astype(jnp.bfloat16)
    for d in range(3):
        total = f32_dot(left_ref[d * slab : (d + 1) * slab, :], right_ref[...])
        own_ref[d] = total[0:part]
        for k in range(1, quads):
            send_refs[k - 1][d] = total[k * part : (k + 1) * part].astype(jnp.bfloat16)


def relaid_kernel(pieces_count, *refs):
    pieces = refs[:pieces_count]
    place_ref, out_ref = refs[pieces_count:]
    groups, size, _ = place_ref.shape
    own_groups = groups // QUAD
    seat = seat_and_quad()[0]
    for h in range(own_groups):
        group = seat * own_groups + h
        rows = group_rows(pieces, pl.multiple_of(group * GRANULE, GRANULE))
        moved = f32_dot(place_ref[group], rows, (((0,), (0,)), ((), ())))
        out_ref[h * size : (h + 1) * size, :] = moved.astype(jnp.bfloat16)


def sum_kernel(own_ref, *refs):
    out_ref = refs[-1]
    columns = own_ref.shape[2]
    for d in range(3):
        total = own_ref[d]
        for ref in refs[:-1]:
            total = total + ref[d].astype(jnp.float32)
        out_ref[:, d * columns : (d + 1) * columns] = total


def by_quads(basis, elem_owned, node_order, geometry, deriv):
    width = lax.axis_size("rows")
    local_rows, columns = basis.shape
    local_elems = local_rows // NP
    repeats = NP // width
    quads = width // QUAD
    block = QUAD * local_elems * repeats
    groups = block // GRANULE
    size = width * GRANULE
    part = columns // width
    slab = quads * part
    owned = elem_owned[None, :]

    packed = call(
        functools.partial(pack_kernel, quads, repeats),
        [near((block, columns), jnp.bfloat16)] * quads,
        (owned, basis),
        2 * local_rows * local_rows * columns,
    )

    def flip(bits):
        return [(i, i ^ bits) for i in range(width)]

    arrived = [packed[0]] + [lax.ppermute(packed[k], "rows", flip(QUAD * k)) for k in range(1, quads)]
    pieces = []
    for k in range(quads):
        across = lax.ppermute(arrived[k], "rows", flip(2))
        beside = lax.ppermute(arrived[k], "rows", flip(1))
        corner = lax.ppermute(across, "rows", flip(1))
        pieces += [arrived[k], beside, across, corner]

    matrix, scale, place = call(
        functools.partial(prepare_kernel, width, repeats),
        [
            near((groups, 3, size, size), jnp.bfloat16),
            near((groups, 3, size), jnp.float32),
            near((groups, size, size), jnp.bfloat16),
        ],
        (owned, node_order.T, geometry.T, deriv),
        groups * 3 * 4 * size**3,
    )
    block_shape = (3, part, columns)
    sums = call(
        functools.partial(product_kernel, width, quads),
        [near(block_shape, jnp.float32)] + [near(block_shape, jnp.bfloat16)] * (quads - 1),
        (*pieces, matrix, scale),
        2 * width * block * slab * 3 * (columns + size) + 2 * width * block * slab * columns,
        scratch=[
            pltpu.VMEM((3 * slab, width * block), jnp.bfloat16),
            pltpu.VMEM((width * block, columns), jnp.bfloat16),
        ],
    )
    landed = [lax.ppermute(sums[k], "rows", flip(QUAD * k)) for k in range(1, quads)]
    (relaid,) = call(
        functools.partial(relaid_kernel, width),
        [jax.ShapeDtypeStruct((local_rows, columns), jnp.bfloat16)],
        (*pieces, place),
        2 * local_rows * size * columns,
    )
    (reduced,) = call(
        sum_kernel,
        [jax.ShapeDtypeStruct((part, 3 * columns), jnp.float32)],
        (sums[0], *landed),
        3 * quads * part * columns,
    )
    return relaid, reduced


def by_rows(basis, elem_owned, node_order, geometry, deriv):
    width_rows = lax.axis_size("rows")
    position = lax.axis_index("rows")
    local_rows, columns = basis.shape
    local_elems = local_rows // NP
    classes = max(1, width_rows // NP)
    repeats = max(1, NP // width_rows)
    class_table = elem_owned.reshape(width_rows, local_elems // classes, classes)
    my_class = position // NP % classes
    chosen = lax.dynamic_index_in_dim(class_table, my_class, axis=2, keepdims=False)
    offsets = position % NP + width_rows * jnp.arange(repeats, dtype=jnp.int32)
    global_node = NP * chosen[:, :, None] + offsets[None, None, :]
    local_index = ((global_node - position) // width_rows).reshape(-1)
    outgoing = basis[local_index]
    arrived = lax.all_to_all(outgoing, "rows", split_axis=0, concat_axis=0, tiled=True)
    my_elems = lax.dynamic_slice_in_dim(elem_owned, position * local_elems, local_elems)
    my_orders = node_order[my_elems]
    my_nodes = NP * my_elems[:, None] + my_orders
    source = my_nodes % width_rows
    within = (jnp.arange(local_elems, dtype=jnp.int32) // classes)[:, None]
    slot_index = (source * (local_elems // classes) + within) * repeats + my_orders // width_rows
    relaid = arrived[slot_index.reshape(-1)]
    geo_rows = geometry[my_elems]
    image = jnp.einsum(
        "dkl,elc->ekdc",
        deriv,
        relaid.reshape(local_elems, NP, columns),
        preferred_element_type=jnp.float32,
    )
    image = (image * geo_rows[:, None, :, None]).astype(jnp.bfloat16)
    image = image.reshape(local_rows, 3 * columns)
    reduced = lax.psum_scatter(
        lax.dot_general(
            relaid, image, (((0,), (0,)), ((), ())), preferred_element_type=jnp.float32
        ),
        "rows",
        scatter_dimension=0,
        tiled=True,
    )
    return (relaid, reduced)


def solution(mesh):
    width = mesh.shape["rows"]
    local = by_quads if width % QUAD == 0 and NP % width == 0 else by_rows
    return jax.shard_map(
        local,
        mesh=mesh,
        in_specs=(
            P(("groups", "rows"), None),
            P("groups"),
            P("groups", None),
            P("groups", None),
            P(),
        ),
        out_specs=(P(("groups", "rows"), None), P(("groups", "rows"), None)),
        check_vma=False,
    )
```

```python
import functools
import math

import jax
import jax.numpy as jnp
from jax import lax
from jax.experimental import pallas as pl
from jax.experimental.pallas import tpu as pltpu
from jax.sharding import PartitionSpec as P

NP = 64
QUAD = 4
GRANULE = 16
KERNEL_BYTES = 16 * 2**20
LANES = (((1,), (1,)), ((), ()))


def whole_vmem(count):
    return [pl.BlockSpec(memory_space=pltpu.VMEM)] * count


def f32_dot(left, right, dims=(((1,), (0,)), ((), ()))):
    return lax.dot_general(left, right, dims, preferred_element_type=jnp.float32)


def near(shape, dtype):
    return pltpu.VMEM(shape, dtype)


def size_of(array):
    return math.prod(array.shape) * jnp.dtype(array.dtype).itemsize


def call(kernel, outs, args, flops, scratch=(), far=0):
    moved = sum(size_of(a) for a in (*args, *outs))
    return pl.pallas_call(
        kernel,
        out_shape=outs,
        in_specs=[pl.BlockSpec(memory_space=pltpu.HBM)] * far + whole_vmem(len(args) - far),
        out_specs=whole_vmem(len(outs)),
        scratch_shapes=scratch,
        compiler_params=pltpu.CompilerParams(vmem_limit_bytes=KERNEL_BYTES),
        cost_estimate=pl.CostEstimate(flops=flops, bytes_accessed=moved, transcendentals=0),
    )(*(pltpu.with_memory_space_constraint(a, pltpu.HBM if i < far else pltpu.VMEM) for i, a in enumerate(args)))


def one(mask):
    return mask.astype(jnp.float32).astype(jnp.bfloat16)


def iota(shape, axis):
    return lax.broadcasted_iota(jnp.int32, shape, axis)


def seat_and_quad():
    position = lax.axis_index("rows").astype(jnp.int32)
    return position % QUAD, position // QUAD


def fetch(far, near_refs, sems):
    copies = [pltpu.make_async_copy(src, dst, sems.at[i]) for i, (src, dst) in enumerate(zip(far, near_refs))]
    for copy in copies:
        copy.start()
    return copies


def pack_kernel(quads, repeats, owned_far, basis_far, *refs):
    *out_refs, owned_ref, basis_ref, sems = refs
    owned_copy, basis_copy = fetch((owned_far, basis_far), (owned_ref, basis_ref), sems)
    total = owned_ref.shape[1]
    rows = basis_ref.shape[0]
    block = rows // quads
    quad_elems = block // repeats
    quad = seat_and_quad()[1]
    row = iota((rows, total), 0)
    wanted = ((row // block) ^ quad) * quad_elems + row % block // repeats
    pick = one(wanted == iota((rows, total), 1))
    owned_copy.wait()
    owned = owned_ref[...].astype(jnp.float32)
    high = jnp.floor(owned / NP)
    parts = jnp.concatenate([owned - NP * high, high, jnp.zeros((6, total), jnp.float32)], axis=0)
    found = f32_dot(pick, parts.astype(jnp.bfloat16), LANES)
    elem = (found[:, 0:1] + NP * found[:, 1:2]).astype(jnp.int32)
    index = elem * repeats + iota((rows, 1), 0) % repeats
    onehot = one(index == iota((rows, rows), 1))
    basis_copy.wait()
    moved = f32_dot(onehot, basis_ref[...]).astype(jnp.bfloat16)
    for k in range(quads):
        out_refs[k][...] = moved[k * block : (k + 1) * block]


def prepare_kernel(width, repeats, *refs):
    far, (matrix_ref, scale_ref, place_ref), (*mine, sems) = refs[:4], refs[4:7], refs[7:]
    owned_ref, order_ref, geo_ref, deriv_ref = mine
    for copy in fetch(far, mine, sems):
        copy.wait()
    groups, _, size, _ = matrix_ref.shape
    total = owned_ref.shape[1]
    elems = size // NP
    quad_elems = groups * elems
    seat, quad = seat_and_quad()
    first = quad * quad_elems
    owner = one(iota((total, total), 0) == owned_ref[...])
    row = iota((quad_elems, total), 0)
    wanted = one(first + row % groups * elems + row // groups == iota((quad_elems, total), 1))
    chosen = f32_dot(wanted, owner, LANES).astype(jnp.bfloat16)
    table = order_ref[...].astype(jnp.float32).astype(jnp.bfloat16)
    orders = f32_dot(chosen, table, LANES).astype(jnp.int32)
    orders = jnp.concatenate([orders[e * groups : (e + 1) * groups] for e in range(elems)], axis=1)
    source = orders % width
    inside = iota((groups, size), 1) // NP * repeats + orders // width
    slot = (((source // QUAD) ^ quad) * QUAD + ((source % QUAD) ^ seat)) * GRANULE + inside

    lane = iota((total, size), 1)
    geo = geo_ref[...]
    top = geo.astype(jnp.bfloat16).astype(jnp.float32)
    middle = (geo - top).astype(jnp.bfloat16).astype(jnp.float32)
    parts = jnp.concatenate([top, middle, geo - top - middle], axis=0).astype(jnp.bfloat16)
    by_slot = f32_dot(parts, owner, (((1,), (0,)), ((), ()))).astype(jnp.bfloat16)
    for g in range(groups):
        stored = first + g * elems + lane % GRANULE // repeats
        spread = f32_dot(by_slot, one(iota((total, size), 0) == stored))
        scale_ref[g] = spread[0:3] + spread[3:6] + spread[6:9]

    same = iota((size, size), 0) // NP == iota((size, size), 1) // NP
    blocks = []
    for d in range(3):
        wide = jnp.concatenate([deriv_ref[d].astype(jnp.float32)] * elems, axis=1)
        tall = jnp.concatenate([wide] * elems, axis=0)
        blocks.append(jnp.where(same, tall, 0.0).astype(jnp.bfloat16))
    for g in range(groups):
        onehot = one(iota((size, size), 0) == slot[g : g + 1, :])
        place_ref[g] = onehot
        for d in range(3):
            half = f32_dot(onehot, blocks[d]).astype(jnp.bfloat16)
            matrix_ref[g, d] = f32_dot(half, onehot, LANES).astype(jnp.bfloat16)


def group_rows(pieces, start):
    return jnp.concatenate([piece[pl.ds(start, GRANULE), :] for piece in pieces], axis=0)


def product_kernel(pieces_count, quads, *refs):
    pieces = refs[:pieces_count]
    matrix_ref, scale_ref = refs[pieces_count : pieces_count + 2]
    own_ref, *send_refs = refs[pieces_count + 2 : pieces_count + 2 + quads]
    left_ref, right_ref = refs[pieces_count + 2 + quads :]
    groups, _, size, _ = matrix_ref.shape
    _, part, columns = own_ref.shape
    slab = quads * part
    seat, quad = seat_and_quad()
    row = iota((slab, columns), 0)
    target = (((row // part) ^ quad) * QUAD + seat) * part + row % part
    select = one(target == iota((slab, columns), 1))
    for g in range(groups):
        rows = group_rows(pieces, g * GRANULE)
        right_ref[g * size : (g + 1) * size, :] = rows
        chosen = f32_dot(select, rows, LANES).astype(jnp.bfloat16)
        for d in range(3):
            left = f32_dot(chosen, matrix_ref[g, d]) * scale_ref[g, d : d + 1, :]
            left_ref[d * slab : (d + 1) * slab, g * size : (g + 1) * size] = left.astype(jnp.bfloat16)
    for d in range(3):
        total = f32_dot(left_ref[d * slab : (d + 1) * slab, :], right_ref[...])
        own_ref[d] = total[0:part]
        for k in range(1, quads):
            send_refs[k - 1][d] = total[k * part : (k + 1) * part].astype(jnp.bfloat16)


def relaid_kernel(pieces_count, *refs):
    pieces = refs[:pieces_count]
    place_ref, out_ref = refs[pieces_count:]
    groups, size, _ = place_ref.shape
    own_groups = groups // QUAD
    seat = seat_and_quad()[0]
    for h in range(own_groups):
        group = seat * own_groups + h
        rows = group_rows(pieces, pl.multiple_of(group * GRANULE, GRANULE))
        moved = f32_dot(place_ref[group], rows, (((0,), (0,)), ((), ())))
        out_ref[h * size : (h + 1) * size, :] = moved.astype(jnp.bfloat16)


def sum_kernel(own_ref, *refs):
    out_ref = refs[-1]
    columns = own_ref.shape[2]
    for d in range(3):
        total = own_ref[d]
        for ref in refs[:-1]:
            total = total + ref[d].astype(jnp.float32)
        out_ref[:, d * columns : (d + 1) * columns] = total


def by_quads(basis, elem_owned, node_order, geometry, deriv):
    width = lax.axis_size("rows")
    local_rows, columns = basis.shape
    local_elems = local_rows // NP
    repeats = NP // width
    quads = width // QUAD
    block = QUAD * local_elems * repeats
    groups = block // GRANULE
    size = width * GRANULE
    part = columns // width
    slab = quads * part
    owned = elem_owned[None, :]

    packed = call(
        functools.partial(pack_kernel, quads, repeats),
        [near((block, columns), jnp.bfloat16)] * quads,
        (owned, basis),
        2 * local_rows * local_rows * columns,
        scratch=[
            pltpu.VMEM(owned.shape, owned.dtype),
            pltpu.VMEM(basis.shape, basis.dtype),
            pltpu.SemaphoreType.DMA((2,)),
        ],
        far=2,
    )

    def flip(bits):
        return [(i, i ^ bits) for i in range(width)]

    def send(array, bits):
        return lax.ppermute(array, "rows", flip(bits))

    arrived = [packed[0]] + [send(packed[k], QUAD * k) for k in range(1, quads)]
    pieces = []
    for k in range(quads):
        across = send(arrived[k], 2)
        beside = send(arrived[k], 1)
        corner = send(across, 1)
        pieces += [arrived[k], beside, across, corner]

    raw = (owned, node_order.T, geometry.T, deriv)
    matrix, scale, place = call(
        functools.partial(prepare_kernel, width, repeats),
        [
            near((groups, 3, size, size), jnp.bfloat16),
            near((groups, 3, size), jnp.float32),
            near((groups, size, size), jnp.bfloat16),
        ],
        raw,
        groups * 3 * 4 * size**3,
        scratch=[*(pltpu.VMEM(a.shape, a.dtype) for a in raw), pltpu.SemaphoreType.DMA((len(raw),))],
        far=len(raw),
    )
    block_shape = (3, part, columns)
    sums = call(
        functools.partial(product_kernel, width, quads),
        [near(block_shape, jnp.float32)] + [near(block_shape, jnp.bfloat16)] * (quads - 1),
        (*pieces, matrix, scale),
        2 * width * block * slab * 3 * (columns + size) + 2 * width * block * slab * columns,
        scratch=[
            pltpu.VMEM((3 * slab, width * block), jnp.bfloat16),
            pltpu.VMEM((width * block, columns), jnp.bfloat16),
        ],
    )
    landed = [send(sums[k], QUAD * k) for k in range(1, quads)]
    (relaid,) = call(
        functools.partial(relaid_kernel, width),
        [jax.ShapeDtypeStruct((local_rows, columns), jnp.bfloat16)],
        (*pieces, place),
        2 * local_rows * size * columns,
    )
    (reduced,) = call(
        sum_kernel,
        [jax.ShapeDtypeStruct((part, 3 * columns), jnp.float32)],
        (sums[0], *landed),
        3 * quads * part * columns,
    )
    return relaid, reduced


def by_rows(basis, elem_owned, node_order, geometry, deriv):
    width_rows = lax.axis_size("rows")
    position = lax.axis_index("rows")
    local_rows, columns = basis.shape
    local_elems = local_rows // NP
    classes = max(1, width_rows // NP)
    repeats = max(1, NP // width_rows)
    class_table = elem_owned.reshape(width_rows, local_elems // classes, classes)
    my_class = position // NP % classes
    chosen = lax.dynamic_index_in_dim(class_table, my_class, axis=2, keepdims=False)
    offsets = position % NP + width_rows * jnp.arange(repeats, dtype=jnp.int32)
    global_node = NP * chosen[:, :, None] + offsets[None, None, :]
    local_index = ((global_node - position) // width_rows).reshape(-1)
    outgoing = basis[local_index]
    arrived = lax.all_to_all(outgoing, "rows", split_axis=0, concat_axis=0, tiled=True)
    my_elems = lax.dynamic_slice_in_dim(elem_owned, position * local_elems, local_elems)
    my_orders = node_order[my_elems]
    my_nodes = NP * my_elems[:, None] + my_orders
    source = my_nodes % width_rows
    within = (jnp.arange(local_elems, dtype=jnp.int32) // classes)[:, None]
    slot_index = (source * (local_elems // classes) + within) * repeats + my_orders // width_rows
    relaid = arrived[slot_index.reshape(-1)]
    geo_rows = geometry[my_elems]
    image = jnp.einsum(
        "dkl,elc->ekdc",
        deriv,
        relaid.reshape(local_elems, NP, columns),
        preferred_element_type=jnp.float32,
    )
    image = (image * geo_rows[:, None, :, None]).astype(jnp.bfloat16)
    image = image.reshape(local_rows, 3 * columns)
    reduced = lax.psum_scatter(
        lax.dot_general(
            relaid, image, (((0,), (0,)), ((), ())), preferred_element_type=jnp.float32
        ),
        "rows",
        scatter_dimension=0,
        tiled=True,
    )
    return (relaid, reduced)


def solution(mesh):
    width = mesh.shape["rows"]
    quads = width // QUAD
    fast = quads > 1 and width % QUAD == 0 and NP % width == 0

    def local(*args):
        return (by_quads if fast else by_rows)(*args)

    return jax.shard_map(
        local,
        mesh=mesh,
        in_specs=(
            P(("groups", "rows"), None),
            P("groups"),
            P("groups", None),
            P("groups", None),
            P(),
        ),
        out_specs=(P(("groups", "rows"), None), P(("groups", "rows"), None)),
        check_vma=False,
    )
```
